512 devices in a mesh: section: 8 (over z_lo), dp: 16 (over x, z_hi, core), tensor: 4 (over y).
Axes of the slice: x: 4, y: 4, z: 16 (z_hi: 2, z_lo: 8; z = z_hi * 8 + z_lo), core: 2. Of those that a mesh axis runs over, the one named last changes fastest.
Arguments:
- norm_in: bfloat16 [8, 2048, 8192], P('section', 'dp', 'tensor'), may hold values from -20 to 20
- query_grad: bfloat16 [8, 2048, 4096], P('section', 'dp', 'tensor'), may hold values from -20 to 20
- attn_out: bfloat16 [8, 2048, 4096], P('section', 'dp', 'tensor'), may hold values from -20 to 20
- handed: bfloat16 [8, 2048, 8192], P('section', 'dp', 'tensor'), may hold values from -20 to 20
- sketch_q: bfloat16 [8, 64, 4096], P('section', None, 'tensor'), may hold values from -6 to 6
- sketch_o: bfloat16 [8, 64, 8192], P('section', None, 'tensor'), may hold values from -6 to 6
Outputs:
- lora_b_q: bfloat16 [8, 64, 8192], P('section', None, 'tensor')
- lora_a_q: float32 [8, 64, 4096], P('section', None, 'tensor')
- lora_b_o: bfloat16 [8, 64, 4096], P('section', None, 'tensor')
- lora_a_o: float32 [8, 64, 8192], P('section', None, 'tensor')
The draws below stay inside these ranges and needn't reach their ends.
All inputs are finite; a program needn't handle non-finite values.
Results may differ from the reference program's by a relative error of at most 0.03.
Values may be sent and summed in bfloat16 or wider, within the bound.
A program may use at most 64 MiB of HBM per device.

```python
import math
import jax
import jax.numpy as jnp
from jax import lax

D = 8192
HQ = 4096
RANK = 64
POWER = 2
TOK_DEV = 128
TOKENS = 2048
SECTIONS = 8
N_DP = 16


def scaled_field(key, full_shape):
    key_rows, key_noise = jax.random.split(key, 2)
    columns = full_shape[-1]
    col_scale = jnp.exp(jnp.arange(columns, dtype=jnp.float32) * (math.log(3.0) / (columns - 1)))
    row_scale = jnp.exp(jax.random.uniform(key_rows, full_shape[:-1] + (1,), minval=0.0, maxval=math.log(2.5)))
    noise = jnp.clip(jax.random.normal(key_noise, full_shape), -6.0, 6.0)
    return (0.3 * noise * row_scale * col_scale).astype(jnp.bfloat16)


def draw_norm_in(key, part):
    return scaled_field(jax.random.fold_in(key, 11), (SECTIONS, TOKENS, D))


def draw_query_grad(key, part):
    return scaled_field(jax.random.fold_in(key, 12), (SECTIONS, TOKENS, HQ))


def draw_attn_out(key, part):
    return scaled_field(jax.random.fold_in(key, 13), (SECTIONS, TOKENS, HQ))


def draw_handed(key, part):
    return scaled_field(jax.random.fold_in(key, 14), (SECTIONS, TOKENS, D))


def block_scale(rng, dims, pieces, low, top_value):
    def one(position, parts):
        steps = jax.random.uniform(jax.random.fold_in(jax.random.fold_in(rng, 6), position), (parts,), jnp.float32, low / len(pieces), top_value / len(pieces))
        return jnp.repeat(jnp.exp(steps), dims[position] // parts).reshape((-1,) + (1,) * (len(dims) - position - 1))

    gain = one(*pieces[0])
    for cut in pieces[1:]:
        gain = gain * one(*cut)
    return gain


def gaussian(key, extent, spread, bound, pieces=(), held_as=jnp.bfloat16):
    drawn = spread * jax.random.normal(key, extent, jnp.float32)
    if pieces:
        drawn = drawn * block_scale(key, extent, pieces, -0.22, 0.18)
    return jnp.clip(drawn, -bound, bound).astype(held_as)


def setup_inputs(seed: int = 0) -> dict:
    seeds = jax.random.split(jax.random.key(seed), 7)
    norm_in = draw_norm_in(jax.random.fold_in(seeds[6], 71), 0)
    query_grad = draw_query_grad(jax.random.fold_in(seeds[6], 71), 0)
    attn_out = draw_attn_out(jax.random.fold_in(seeds[6], 71), 0)
    handed = draw_handed(jax.random.fold_in(seeds[6], 71), 0)
    sketch_q = gaussian(seeds[4], (SECTIONS, RANK, HQ), 1.0, 6.0, ((0, 8), (2, 4)))
    sketch_o = gaussian(seeds[5], (SECTIONS, RANK, D), 1.0, 6.0, ((0, 8), (2, 4)))
    return {"norm_in": norm_in, "query_grad": query_grad, "attn_out": attn_out, "handed": handed, "sketch_q": sketch_q, "sketch_o": sketch_o}


precise = lax.Precision.HIGHEST

def orthonormal(row_block):
    gram_rows = jnp.dot(row_block.astype(jnp.float32), row_block.T.astype(jnp.float32), precision=precise, preferred_element_type=jnp.float32)
    low_factor = jnp.linalg.cholesky(gram_rows)
    solved = lax.linalg.triangular_solve(low_factor, row_block, left_side=True, lower=True)
    return solved.astype(jnp.bfloat16)

def factor(basis, matrix):
    return jnp.dot(basis.astype(jnp.float32), matrix.T.astype(jnp.float32), preferred_element_type=jnp.float32).astype(jnp.bfloat16)

def summed(token_rows, matrix):
    token_blocks = token_rows.reshape(RANK, N_DP, TOK_DEV).transpose(1, 0, 2)
    matrix_blocks = matrix.reshape(N_DP, TOK_DEV, matrix.shape[1])

    def block_product(two_parts):
        return jnp.dot(two_parts[0].astype(jnp.float32), two_parts[1].astype(jnp.float32), preferred_element_type=jnp.float32).astype(jnp.bfloat16)
    partial_value = lax.map(block_product, (token_blocks, matrix_blocks))
    return lax.optimization_barrier(jnp.sum(partial_value.astype(jnp.float32), axis=0))

def adapters(left, right, sketch):
    basis = orthonormal(summed(factor(sketch, right), left))
    for iteration in range(POWER):
        other = orthonormal(summed(factor(basis, left), right))
        basis = orthonormal(summed(factor(other, right), left))
    raw = summed(factor(basis, left), right)
    norm_scale = jnp.sqrt(jnp.mean(raw * raw) + 1e-06)
    return (basis * 16.0, raw / norm_scale)

def reference(norm_in, query_grad, attn_out, handed, sketch_q, sketch_o):
    upstream = jnp.concatenate([handed[1:], handed[:1]], axis=0)

    def per_section(section_items):
        norm_rows, query_rows, attn_rows, up_rows, sketch_a, sketch_b = section_items
        b_query, a_query = adapters(norm_rows, query_rows, sketch_a)
        b_output, a_output = adapters(attn_rows, up_rows, sketch_b)
        return (b_query, a_query, b_output, a_output)
    b_query, a_query, b_output, a_output = lax.map(per_section, (norm_in, query_grad, attn_out, upstream, sketch_q, sketch_o))
    return (b_query, a_query, b_output, a_output)
```

```python
import functools

import jax
import jax.numpy as jnp
from jax import lax
from jax.experimental import pallas as pl
from jax.experimental.pallas import tpu as pltpu
from jax.sharding import PartitionSpec as P

RANK = 64
POWER = 2
STAGES = 2 * POWER + 2
NY = 4
GROUP = 8
MESH = pl.DeviceIdType.MESH
f32 = jnp.float32
bf16 = jnp.bfloat16
precise = lax.Precision.HIGHEST


def dot_rows(a, b):
    return lax.dot_general(a, b, (((1,), (1,)), ((), ())), preferred_element_type=f32)


def eliminate(blocks):
    sub = lax.broadcasted_iota(jnp.int32, (8, 128), 0)

    def one_block(b, rows):
        rows = list(rows)
        live = [jnp.where(p + b < 8, 1.0, 0.0).astype(f32) for p in range(1, 8)]
        for i in range(8):
            row = jnp.broadcast_to(rows[0][i : i + 1, :], (8, 128))
            root = lax.rsqrt(jnp.broadcast_to(row[:, i : i + 1], (8, 128)))
            unit = row * root
            scaled = unit * root
            head = rows[0]
            lower = head - jnp.broadcast_to(head[:, i : i + 1], (8, 128)) * scaled
            for p in range(1, 8):
                column = jnp.broadcast_to(rows[p][:, i : i + 1], (8, 128))
                rows[p] = rows[p] - (column * live[p - 1]) * scaled
            rows[0] = jnp.where(sub == i, unit, jnp.where(sub > i, lower, head))
        rows = [pltpu.roll(r, 120, 1) for r in rows]
        return tuple(rows[1:] + rows[:1])

    return lax.fori_loop(0, 8, one_block, tuple(blocks))


def kernel(
    norm_ref, query_ref, attn_ref, handed_ref, sk_q_ref, sk_o_ref,
    b_q_ref, a_q_ref, b_o_ref, a_o_ref,
    up, y_buf, e_buf, inv_buf, scale_buf, send_w, send_n, recv_w, recv_n, z_w, z_n, all_w, all_n,
    up_sems, y_send, y_recv, rs_send, rs_recv, z_send, z_recv, ag_send, ag_recv, e_send, e_recv,
):
    section = lax.axis_index("section")
    dp = lax.axis_index("dp")
    y = lax.axis_index("tensor")
    sections = lax.axis_size("section")
    x, z, core = dp // 4, (dp // 2) % 2, dp % 2
    me = x * 2 + core
    behind, ahead = (section + sections - 1) % sections, (section + 1) % sections

    def y_peer(r):
        return {"tensor": (y + r) % NY}

    def group_peer(r):
        other = (me + r) % GROUP
        return {"dp": ((other // 2) * 2 + z) * 2 + other % 2}

    z_peer = {"dp": (x * 2 + (1 - z)) * 2 + core}

    barrier = pltpu.get_barrier_semaphore()
    peers = [{"section": behind}, {"section": ahead}, z_peer]
    peers += [y_peer(r) for r in range(1, NY)] + [group_peer(r) for r in range(1, GROUP)]
    for peer in peers:
        pl.semaphore_signal(barrier, inc=1, device_id=peer, device_id_type=MESH)
    pl.semaphore_wait(barrier, len(peers))

    def remote(src, dst, sent, received, peer):
        copy = pltpu.make_async_remote_copy(
            src_ref=src, dst_ref=dst, send_sem=sent, recv_sem=received, device_id=peer, device_id_type=MESH
        )
        copy.start()
        return copy

    pending = []
    shift = remote(handed_ref, up, up_sems.at[0], up_sems.at[1], {"section": behind})
    pending.append(shift)

    def chain(c, left, right, sketch, b_out, a_out):
        for k in range(STAGES):
            before, here = (right, left) if k % 2 == 0 else (left, right)
            wide = here.shape[2] // GROUP
            big = wide == 256
            slot = c * 3 + k // 2
            mine, theirs, z_b, everyone = (
                (send_w, recv_w, z_w, all_w) if big else (send_n, recv_n, z_n, all_n)
            )
            mine, theirs, z_b, everyone = mine.at[slot], theirs.at[slot], z_b.at[slot], everyone.at[slot]
            idx = c * STAGES + k

            if k == 0:
                part = dot_rows(sketch[0], before[0])
                y_buf[idx, y, :RANK, :] = part.astype(bf16)
                span = RANK
            else:
                both = None
                width = before.shape[2] // GROUP
                for j in range(GROUP):
                    piece = last[j]
                    stacked = jnp.concatenate([before[0, :, j * width : (j + 1) * width], piece, piece], axis=0)
                    term = dot_rows(piece, stacked)
                    both = term if both is None else both + term
                y_buf[idx, y, :RANK, :] = both[:, :128].astype(bf16)
                gram = both[:, 128:]
                high = gram.astype(bf16)
                rest = (gram - high.astype(f32)).astype(bf16)
                lane = lax.broadcasted_iota(jnp.int32, (RANK, 128), 1)
                y_buf[idx, y, RANK:, :] = jnp.where(lane < RANK, high.astype(f32), rest.astype(f32)).astype(bf16)
                span = 2 * RANK
            own = y_buf.at[idx, y, pl.ds(0, span)]
            copies = [
                remote(own, own, y_send.at[idx, r - 1], y_recv.at[idx, r - 1], y_peer(r)) for r in range(1, NY)
            ]
            pending.extend(copies)
            yield
            for copy in copies:
                copy.wait_recv()
            token_sum = y_buf[idx, 0, :RANK, :].astype(f32)
            for j in range(1, NY):
                token_sum = token_sum + y_buf[idx, j, :RANK, :].astype(f32)
            blocks = None
            if k > 0:
                packed = y_buf[idx, 0, RANK:, :].astype(f32)
                for j in range(1, NY):
                    packed = packed + y_buf[idx, j, RANK:, :].astype(f32)
                gram = packed + pltpu.roll(packed, RANK, 1)
                line = lax.broadcasted_iota(jnp.int32, (RANK, 128), 0)
                lane = lax.broadcasted_iota(jnp.int32, (RANK, 128), 1)
                diagonal = jnp.where(line == lane, gram, 0.0)
                by_row = lax.rsqrt(jnp.sum(diagonal, axis=1, keepdims=True))
                column_diagonal = jnp.where((line == lane) | (line + RANK == lane), gram, 0.0)
                by_lane = lax.rsqrt(jnp.sum(column_diagonal, axis=0, keepdims=True))
                token_sum = token_sum * by_row
                scaled = gram * by_row * by_lane
                augmented = jnp.where(lane < RANK, scaled, jnp.where(line + RANK == lane, 1.0, 0.0))
                inv_buf[c] = augmented
                scale_buf[c] = jnp.broadcast_to(by_lane, (8, 128))
            rows = token_sum.astype(bf16)
            for j in range(GROUP):
                piece = jnp.dot(rows, here[0, :, j * wide : (j + 1) * wide], preferred_element_type=f32)
                mine[j] = piece.astype(bf16)
            copies = []
            for r in range(1, GROUP):
                other = (me + r) % GROUP
                copies.append(
                    remote(
                        mine.at[other], theirs.at[me], rs_send.at[idx, r - 1], rs_recv.at[idx, r - 1], group_peer(r)
                    )
                )
            pending.extend(copies)
            theirs[me] = mine[me]
            yield
            for copy in copies:
                copy.wait_recv()
            total = theirs[0].astype(f32)
            for j in range(1, GROUP):
                total = total + theirs[j].astype(f32)
            z_b[0] = total.astype(bf16)
            copy = remote(z_b.at[0], z_b.at[1], z_send.at[idx], z_recv.at[idx], z_peer)
            pending.append(copy)
            if k > 0:
                reduced = eliminate([inv_buf[c, 8 * p : 8 * p + 8, :] for p in range(8)])
                for p in range(8):
                    inv_buf[c, 8 * p : 8 * p + 8, :] = reduced[p]
                if k == STAGES - 1:
                    inverse = inv_buf[c][:, :RANK] * scale_buf[c][:1, :RANK]
                    width = before.shape[2] // GROUP
                    for j in range(GROUP):
                        basis = jnp.dot(
                            inverse, last[j].astype(f32), precision=precise, preferred_element_type=f32
                        )
                        b_out[0, :, j * width : (j + 1) * width] = (basis.astype(bf16).astype(f32) * 16.0).astype(bf16)
            yield
            copy.wait_recv()
            total = z_b[0].astype(f32) + z_b[1].astype(f32)
            if k > 0:
                total = jnp.dot(inv_buf[c][:, :RANK], total, precision=precise, preferred_element_type=f32)
            everyone[me] = total.astype(bf16)
            own = everyone.at[me]
            copies = [
                remote(own, own, ag_send.at[idx, r - 1], ag_recv.at[idx, r - 1], group_peer(r))
                for r in range(1, GROUP)
            ]
            pending.extend(copies)
            yield
            for copy in copies:
                copy.wait_recv()
            last = everyone
        energy = None
        for j in range(GROUP):
            value = last[j].astype(f32)
            value = value * value
            for i in range(8):
                for lanes in range(0, value.shape[1], 128):
                    term = value[8 * i : 8 * i + 8, lanes : lanes + 128]
                    energy = term if energy is None else energy + term
        e_buf[c, y] = energy
        own = e_buf.at[c, y]
        copies = [remote(own, own, e_send.at[c, r - 1], e_recv.at[c, r - 1], y_peer(r)) for r in range(1, NY)]
        pending.extend(copies)
        yield
        for copy in copies:
            copy.wait_recv()
        energy = e_buf[c, 0] + e_buf[c, 1] + e_buf[c, 2] + e_buf[c, 3]
        energy = jnp.sum(jnp.sum(energy, axis=1, keepdims=True), axis=0, keepdims=True)
        columns = GROUP * wide * NY
        factor = 1.0 / jnp.sqrt(energy / (RANK * columns) + 1e-06)
        for j in range(GROUP):
            a_out[0, :, j * wide : (j + 1) * wide] = last[j].astype(f32) * factor
        yield

    first = chain(0, norm_ref, query_ref, sk_q_ref, b_q_ref, a_q_ref)
    second = chain(1, attn_ref, up, sk_o_ref, b_o_ref, a_o_ref)
    for _ in range(3):
        next(first)
    shift.wait_recv()
    next(second)
    order = []
    for _ in range(STAGES - 1):
        order += [1, 0, 1, 0, 0, 1, 0, 1]
    order += [1, 0, 1, 0, 0, 1, 1, 1]
    chains = (first, second)
    for which in order:
        next(chains[which])
    for copy in pending:
        copy.wait_send()


def body(*operands):
    norm_in, query_grad, attn_out, handed, sketch_q, sketch_o = operands
    dim, features = norm_in.shape[2], query_grad.shape[2]
    tokens = norm_in.shape[1]
    vmem = pl.BlockSpec(memory_space=pltpu.VMEM)
    wide, narrow = dim // GROUP, features // GROUP
    dma = pltpu.SemaphoreType.DMA
    n = 2 * STAGES
    out_shape = (
        jax.ShapeDtypeStruct((1, RANK, dim), bf16),
        jax.ShapeDtypeStruct((1, RANK, features), f32),
        jax.ShapeDtypeStruct((1, RANK, features), bf16),
        jax.ShapeDtypeStruct((1, RANK, dim), f32),
    )
    scratch = [
        pltpu.VMEM((1, tokens, dim), bf16),
        pltpu.VMEM((n, NY, 2 * RANK, 128), bf16),
        pltpu.VMEM((2, NY, 8, 128), f32),
        pltpu.VMEM((2, RANK, 128), f32),
        pltpu.VMEM((2, 8, 128), f32),
        pltpu.VMEM((STAGES, GROUP, RANK, wide), bf16),
        pltpu.VMEM((STAGES, GROUP, RANK, narrow), bf16),
        pltpu.VMEM((STAGES, GROUP, RANK, wide), bf16),
        pltpu.VMEM((STAGES, GROUP, RANK, narrow), bf16),
        pltpu.VMEM((STAGES, 2, RANK, wide), bf16),
        pltpu.VMEM((STAGES, 2, RANK, narrow), bf16),
        pltpu.VMEM((STAGES, GROUP, RANK, wide), bf16),
        pltpu.VMEM((STAGES, GROUP, RANK, narrow), bf16),
        dma((2,)),
        dma((n, NY - 1)),
        dma((n, NY - 1)),
        dma((n, GROUP - 1)),
        dma((n, GROUP - 1)),
        dma((n,)),
        dma((n,)),
        dma((n, GROUP - 1)),
        dma((n, GROUP - 1)),
        dma((2, NY - 1)),
        dma((2, NY - 1)),
    ]
    return pl.pallas_call(
        kernel,
        out_shape=out_shape,
        in_specs=[vmem] * 6,
        out_specs=(vmem,) * 4,
        scratch_shapes=scratch,
        compiler_params=pltpu.CompilerParams(
            collective_id=0, has_side_effects=True, vmem_limit_bytes=40 * 1024 * 1024
        ),
        name="adapters",
    )(*operands)


def solution(mesh):
    row = P("section", "dp", "tensor")
    thin = P("section", None, "tensor")
    return jax.shard_map(
        body,
        mesh=mesh,
        in_specs=(row, row, row, row, thin, thin),
        out_specs=(thin, thin, thin, thin),
        check_vma=False,
    )
```

```python
import functools

import jax
import jax.numpy as jnp
from jax import lax
from jax.experimental import pallas as pl
from jax.experimental.pallas import tpu as pltpu
from jax.sharding import PartitionSpec as P

RANK = 64
POWER = 2
STAGES = 2 * POWER + 2
NY = 4
GROUP = 8
MESH = pl.DeviceIdType.MESH
f32 = jnp.float32
bf16 = jnp.bfloat16
precise = lax.Precision.HIGHEST


def dot_rows(a, b):
    return lax.dot_general(a, b, (((1,), (1,)), ((), ())), preferred_element_type=f32)


def eliminate(blocks):
    sub = lax.broadcasted_iota(jnp.int32, (8, 128), 0)

    def across(value, i):
        return jnp.broadcast_to(value[:, i : i + 1], (8, 128))

    def down(value, i):
        return jnp.broadcast_to(value[i : i + 1, :], (8, 128))

    def one_block(b, rows):
        rows = list(rows)
        work = done = rows[0]
        columns = [across(work, i) for i in range(8)]
        for i in range(8):
            pivot = down(columns[i], i)
            root = lax.rsqrt(pivot)
            row = down(work, i)
            done = jnp.where(sub == i, row * root, done)
            step = jnp.where(sub == i, pivot - 1.0, columns[i]) * (root * root)
            for j in range(i + 1, 8):
                columns[j] = columns[j] - down(columns[j], i) * step
            work = work - row * step
        solved = [down(work, i) for i in range(8)]
        for p in range(1, 8):
            change = across(rows[p], 0) * solved[0]
            for i in range(1, 8):
                change = change + across(rows[p], i) * solved[i]
            live = jnp.where(p + b < 8, 1.0, 0.0).astype(f32)
            rows[p] = rows[p] - change * live
        rows[0] = done
        rows = [pltpu.roll(r, 120, 1) for r in rows]
        return tuple(rows[1:] + rows[:1])

    return lax.fori_loop(0, 8, one_block, tuple(blocks))


def kernel(
    norm_hbm, query_hbm, attn_hbm, handed_hbm, sk_q_hbm, sk_o_hbm,
    b_q_ref, a_q_ref, b_o_ref, a_o_ref,
    norm_ref, query_ref, attn_ref, sk_q_ref, sk_o_ref, up, y_buf, e_buf, inv_buf, scale_buf, send_w, send_n, recv_w, recv_n, z_w, z_n, all_w, all_n,
    up_sems, y_send, y_recv, rs_send, rs_recv, z_send, z_recv, ag_send, ag_recv, e_send, e_recv, in_sems,
):
    section = lax.axis_index("section")
    dp = lax.axis_index("dp")
    y = lax.axis_index("tensor")
    sections = lax.axis_size("section")
    x, z, core = dp // 4, (dp // 2) % 2, dp % 2
    me = x * 2 + core
    behind, ahead = (section + sections - 1) % sections, (section + 1) % sections

    def y_peer(r):
        return {"tensor": (y + r) % NY}

    def group_peer(r):
        other = (me + r) % GROUP
        return {"dp": ((other // 2) * 2 + z) * 2 + other % 2}

    z_peer = {"dp": (x * 2 + (1 - z)) * 2 + core}

    loads = [
        pltpu.make_async_copy(source, target, in_sems.at[i])
        for i, (source, target) in enumerate(
            (
                (query_hbm, query_ref), (sk_q_hbm, sk_q_ref), (norm_hbm, norm_ref),
                (sk_o_hbm, sk_o_ref), (attn_hbm, attn_ref),
            )
        )
    ]
    for load in loads:
        load.start()
    barrier = pltpu.get_barrier_semaphore()
    peers = [{"section": behind}, {"section": ahead}, z_peer]
    peers += [y_peer(r) for r in range(1, NY)] + [group_peer(r) for r in range(1, GROUP)]
    for peer in peers:
        pl.semaphore_signal(barrier, inc=1, device_id=peer, device_id_type=MESH)
    pl.semaphore_wait(barrier, len(peers))

    def remote(src, dst, sent, received, peer):
        copy = pltpu.make_async_remote_copy(
            src_ref=src, dst_ref=dst, send_sem=sent, recv_sem=received, device_id=peer, device_id_type=MESH
        )
        copy.start()
        return copy

    pending = []
    shift = remote(handed_hbm, up, up_sems.at[0], up_sems.at[1], {"section": behind})
    pending.append(shift)
    for load in loads:
        load.wait()

    def chain(c, left, right, sketch, b_out, a_out):
        for k in range(STAGES):
            before, here = (right, left) if k % 2 == 0 else (left, right)
            wide = here.shape[2] // GROUP
            big = wide == 256
            slot = c * 3 + k // 2
            mine, theirs, z_b, everyone = (
                (send_w, recv_w, z_w, all_w) if big else (send_n, recv_n, z_n, all_n)
            )
            mine, theirs, z_b, everyone = mine.at[slot], theirs.at[slot], z_b.at[slot], everyone.at[slot]
            idx = c * STAGES + k

            if k == 0:
                part = dot_rows(sketch[0], before[0])
                y_buf[idx, y, :RANK, :] = part.astype(bf16)
                span = RANK
            else:
                both = None
                width = before.shape[2] // GROUP
                for j in range(GROUP):
                    piece = last[j]
                    stacked = jnp.concatenate([before[0, :, j * width : (j + 1) * width], piece, piece], axis=0)
                    term = dot_rows(piece, stacked)
                    both = term if both is None else both + term
                y_buf[idx, y, :RANK, :] = both[:, :128].astype(bf16)
                gram = both[:, 128:]
                high = gram.astype(bf16)
                rest = (gram - high.astype(f32)).astype(bf16)
                lane = lax.broadcasted_iota(jnp.int32, (RANK, 128), 1)
                y_buf[idx, y, RANK:, :] = jnp.where(lane < RANK, high.astype(f32), rest.astype(f32)).astype(bf16)
                span = 2 * RANK
            own = y_buf.at[idx, y, pl.ds(0, span)]
            copies = [
                remote(own, own, y_send.at[idx, r - 1], y_recv.at[idx, r - 1], y_peer(r)) for r in range(1, NY)
            ]
            pending.extend(copies)
            yield
            for copy in copies:
                copy.wait_recv()
            token_sum = y_buf[idx, 0, :RANK, :].astype(f32)
            for j in range(1, NY):
                token_sum = token_sum + y_buf[idx, j, :RANK, :].astype(f32)
            blocks = None
            if k > 0:
                packed = y_buf[idx, 0, RANK:, :].astype(f32)
                for j in range(1, NY):
                    packed = packed + y_buf[idx, j, RANK:, :].astype(f32)
                gram = packed + pltpu.roll(packed, RANK, 1)
                line = lax.broadcasted_iota(jnp.int32, (RANK, 128), 0)
                lane = lax.broadcasted_iota(jnp.int32, (RANK, 128), 1)
                diagonal = jnp.where(line == lane, gram, 0.0)
                by_row = lax.rsqrt(jnp.sum(diagonal, axis=1, keepdims=True))
                column_diagonal = jnp.where((line == lane) | (line + RANK == lane), gram, 0.0)
                by_lane = lax.rsqrt(jnp.sum(column_diagonal, axis=0, keepdims=True))
                token_sum = token_sum * by_row
                scaled = gram * by_row * by_lane
                augmented = jnp.where(lane < RANK, scaled, jnp.where(line + RANK == lane, 1.0, 0.0))
                inv_buf[c] = augmented
                scale_buf[c] = jnp.broadcast_to(by_lane, (8, 128))
            rows = token_sum.astype(bf16)
            for j in range(GROUP):
                piece = jnp.dot(rows, here[0, :, j * wide : (j + 1) * wide], preferred_element_type=f32)
                mine[j] = piece.astype(bf16)
            copies = []
            for r in range(1, GROUP):
                other = (me + r) % GROUP
                copies.append(
                    remote(
                        mine.at[other], theirs.at[me], rs_send.at[idx, r - 1], rs_recv.at[idx, r - 1], group_peer(r)
                    )
                )
            pending.extend(copies)
            theirs[me] = mine[me]
            yield
            for copy in copies:
                copy.wait_recv()
            total = theirs[0].astype(f32)
            for j in range(1, GROUP):
                total = total + theirs[j].astype(f32)
            z_b[0] = total.astype(bf16)
            copy = remote(z_b.at[0], z_b.at[1], z_send.at[idx], z_recv.at[idx], z_peer)
            pending.append(copy)
            if k > 0:
                reduced = eliminate([inv_buf[c, 8 * p : 8 * p + 8, :] for p in range(8)])
                for p in range(8):
                    inv_buf[c, 8 * p : 8 * p + 8, :] = reduced[p]
                if k == STAGES - 1:
                    inverse = inv_buf[c][:, :RANK] * scale_buf[c][:1, :RANK]
                    width = before.shape[2] // GROUP
                    for j in range(GROUP):
                        basis = jnp.dot(
                            inverse, last[j].astype(f32), precision=precise, preferred_element_type=f32
                        )
                        b_out[0, :, j * width : (j + 1) * width] = (basis.astype(bf16).astype(f32) * 16.0).astype(bf16)
            yield
            copy.wait_recv()
            total = z_b[0].astype(f32) + z_b[1].astype(f32)
            if k > 0:
                total = jnp.dot(inv_buf[c][:, :RANK], total, precision=precise, preferred_element_type=f32)
            everyone[me] = total.astype(bf16)
            own = everyone.at[me]
            copies = [
                remote(own, own, ag_send.at[idx, r - 1], ag_recv.at[idx, r - 1], group_peer(r))
                for r in range(1, GROUP)
            ]
            pending.extend(copies)
            yield
            for copy in copies:
                copy.wait_recv()
            last = everyone
        energy = None
        for j in range(GROUP):
            value = last[j].astype(f32)
            value = value * value
            for i in range(8):
                for lanes in range(0, value.shape[1], 128):
                    term = value[8 * i : 8 * i + 8, lanes : lanes + 128]
                    energy = term if energy is None else energy + term
        e_buf[c, y] = energy
        own = e_buf.at[c, y]
        copies = [remote(own, own, e_send.at[c, r - 1], e_recv.at[c, r - 1], y_peer(r)) for r in range(1, NY)]
        pending.extend(copies)
        yield
        for copy in copies:
            copy.wait_recv()
        energy = e_buf[c, 0] + e_buf[c, 1] + e_buf[c, 2] + e_buf[c, 3]
        energy = jnp.sum(jnp.sum(energy, axis=1, keepdims=True), axis=0, keepdims=True)
        columns = GROUP * wide * NY
        factor = 1.0 / jnp.sqrt(energy / (RANK * columns) + 1e-06)
        for j in range(GROUP):
            a_out[0, :, j * wide : (j + 1) * wide] = last[j].astype(f32) * factor
        yield

    first = chain(0, norm_ref, query_ref, sk_q_ref, b_q_ref, a_q_ref)
    second = chain(1, attn_ref, up, sk_o_ref, b_o_ref, a_o_ref)
    for _ in range(3):
        next(first)
    shift.wait_recv()
    next(second)
    order = []
    for _ in range(STAGES - 1):
        order += [1, 0, 1, 0, 0, 1, 0, 1]
    order += [1, 0, 1, 0, 0, 1, 1, 1]
    chains = (first, second)
    for which in order:
        next(chains[which])
    for copy in pending:
        copy.wait_send()


def body(*operands):
    norm_in, query_grad, attn_out, handed, sketch_q, sketch_o = operands
    dim, features = norm_in.shape[2], query_grad.shape[2]
    tokens = norm_in.shape[1]
    vmem = pl.BlockSpec(memory_space=pltpu.VMEM)
    wide, narrow = dim // GROUP, features // GROUP
    dma = pltpu.SemaphoreType.DMA
    n = 2 * STAGES
    out_shape = (
        jax.ShapeDtypeStruct((1, RANK, dim), bf16),
        jax.ShapeDtypeStruct((1, RANK, features), f32),
        jax.ShapeDtypeStruct((1, RANK, features), bf16),
        jax.ShapeDtypeStruct((1, RANK, dim), f32),
    )
    scratch = [
        pltpu.VMEM(norm_in.shape, bf16),
        pltpu.VMEM(query_grad.shape, bf16),
        pltpu.VMEM(attn_out.shape, bf16),
        pltpu.VMEM(sketch_q.shape, bf16),
        pltpu.VMEM(sketch_o.shape, bf16),
        pltpu.VMEM((1, tokens, dim), bf16),
        pltpu.VMEM((n, NY, 2 * RANK, 128), bf16),
        pltpu.VMEM((2, NY, 8, 128), f32),
        pltpu.VMEM((2, RANK, 128), f32),
        pltpu.VMEM((2, 8, 128), f32),
        pltpu.VMEM((STAGES, GROUP, RANK, wide), bf16),
        pltpu.VMEM((STAGES, GROUP, RANK, narrow), bf16),
        pltpu.VMEM((STAGES, GROUP, RANK, wide), bf16),
        pltpu.VMEM((STAGES, GROUP, RANK, narrow), bf16),
        pltpu.VMEM((STAGES, 2, RANK, wide), bf16),
        pltpu.VMEM((STAGES, 2, RANK, narrow), bf16),
        pltpu.VMEM((STAGES, GROUP, RANK, wide), bf16),
        pltpu.VMEM((STAGES, GROUP, RANK, narrow), bf16),
        dma((2,)),
        dma((n, NY - 1)),
        dma((n, NY - 1)),
        dma((n, GROUP - 1)),
        dma((n, GROUP - 1)),
        dma((n,)),
        dma((n,)),
        dma((n, GROUP - 1)),
        dma((n, GROUP - 1)),
        dma((2, NY - 1)),
        dma((2, NY - 1)),
        dma((5,)),
    ]
    return pl.pallas_call(
        kernel,
        out_shape=out_shape,
        in_specs=[pl.BlockSpec(memory_space=pltpu.HBM)] * 6,
        out_specs=(vmem,) * 4,
        scratch_shapes=scratch,
        compiler_params=pltpu.CompilerParams(
            collective_id=0, has_side_effects=True, vmem_limit_bytes=65800000
        ),
        name="adapters",
    )(*operands)


def solution(mesh):
    row = P("section", "dp", "tensor")
    thin = P("section", None, "tensor")
    return jax.shard_map(
        body,
        mesh=mesh,
        in_specs=(row, row, row, row, thin, thin),
        out_specs=(thin, thin, thin, thin),
        check_vma=False,
    )
```

```python
import functools

import jax
import jax.numpy as jnp
from jax import lax
from jax.experimental import pallas as pl
from jax.experimental.pallas import tpu as pltpu
from jax.sharding import PartitionSpec as P

RANK = 64
POWER = 2
STAGES = 2 * POWER + 2
NY = 4
GROUP = 8
MESH = pl.DeviceIdType.MESH
ORDER = [
    0, 0, 0, 2, 1, 1, 1, 0, 1, 0, 1, 0, 1, 0, 0, 1, 1, 0, 1, 0, 0, 1, 0, 1,
    0, 1, 1, 0, 1, 0, 1, 0, 1, 0, 0, 1, 1, 0, 1, 0, 0, 1, 0, 1, 0, 1, 1, 0,
    1, 0, 1, 0, 1, 0, 1, 0, 1, 0, 0, 1, 0, 1, 1, 1,
]
f32 = jnp.float32
bf16 = jnp.bfloat16
precise = lax.Precision.HIGHEST


def dot_rows(a, b):
    return lax.dot_general(a, b, (((1,), (1,)), ((), ())), preferred_element_type=f32)


def eliminate(blocks):
    sub = lax.broadcasted_iota(jnp.int32, (8, 128), 0)

    def across(value, i):
        return jnp.broadcast_to(value[:, i : i + 1], (8, 128))

    def down(value, i):
        return jnp.broadcast_to(value[i : i + 1, :], (8, 128))

    def one_block(b, rows):
        rows = list(rows)
        work = done = rows[0]
        columns = [across(work, i) for i in range(8)]
        for i in range(8):
            pivot = down(columns[i], i)
            root = lax.rsqrt(pivot)
            row = down(work, i)
            done = jnp.where(sub == i, row * root, done)
            step = jnp.where(sub == i, pivot - 1.0, columns[i]) * (root * root)
            for j in range(i + 1, 8):
                columns[j] = columns[j] - down(columns[j], i) * step
            work = work - row * step
        solved = [down(work, i) for i in range(8)]
        for p in range(1, 8):
            change = across(rows[p], 0) * solved[0]
            for i in range(1, 8):
                change = change + across(rows[p], i) * solved[i]
            live = jnp.where(p + b < 8, 1.0, 0.0).astype(f32)
            rows[p] = rows[p] - change * live
        rows[0] = done
        rows = [pltpu.roll(r, 120, 1) for r in rows]
        return tuple(rows[1:] + rows[:1])

    return lax.fori_loop(0, 8, one_block, tuple(blocks))


def kernel(
    norm_hbm, query_hbm, attn_hbm, handed_hbm, sk_q_hbm, sk_o_hbm,
    b_q_ref, a_q_ref, b_o_ref, a_o_ref,
    norm_ref, query_ref, attn_ref, sk_q_ref, sk_o_ref, up, y_buf, g_buf, e_buf, h_buf, inv_buf, send_w, send_n, recv_w, recv_n, z_w, z_n, all_w, all_n,
    up_sems, y_send, y_recv, g_send, g_recv, rs_send, rs_recv, z_send, z_recv, ag_send, ag_recv, e_send, e_recv, h_send, h_recv, in_sems,
):
    section = lax.axis_index("section")
    dp = lax.axis_index("dp")
    y = lax.axis_index("tensor")
    sections = lax.axis_size("section")
    x, z, core = dp // 4, (dp // 2) % 2, dp % 2
    me = x * 2 + core
    behind, ahead = (section + sections - 1) % sections, (section + 1) % sections

    def y_peer(r):
        return {"tensor": (y + r) % NY}

    def group_peer(r):
        other = (me + r) % GROUP
        return {"dp": ((other // 2) * 2 + z) * 2 + other % 2}

    z_peer = {"dp": (x * 2 + (1 - z)) * 2 + core}

    loads = [
        pltpu.make_async_copy(source, target, in_sems.at[i])
        for i, (source, target) in enumerate(
            (
                (query_hbm, query_ref), (sk_q_hbm, sk_q_ref), (norm_hbm, norm_ref),
                (sk_o_hbm, sk_o_ref), (attn_hbm, attn_ref),
            )
        )
    ]
    for load in loads:
        load.start()
    barrier = pltpu.get_barrier_semaphore()
    peers = [{"section": behind}, {"section": ahead}, z_peer]
    peers += [y_peer(r) for r in range(1, NY)] + [group_peer(r) for r in range(1, GROUP)]
    for peer in peers:
        pl.semaphore_signal(barrier, inc=1, device_id=peer, device_id_type=MESH)

    def remote(src, dst, sent, received, peer):
        copy = pltpu.make_async_remote_copy(
            src_ref=src, dst_ref=dst, send_sem=sent, recv_sem=received, device_id=peer, device_id_type=MESH
        )
        copy.start()
        return copy

    pending = []

    def chain(c, left, right, sketch, b_out, a_out, ready):
        for k in range(STAGES):
            before, here = (right, left) if k % 2 == 0 else (left, right)
            wide = here.shape[2] // GROUP
            width = before.shape[2] // GROUP
            slot = c * 3 + k // 2
            buffers = (send_w, recv_w, z_w, all_w) if wide == 256 else (send_n, recv_n, z_n, all_n)
            mine, theirs, z_b, everyone = (buffer.at[slot] for buffer in buffers)
            idx = c * STAGES + k

            if k == 0:
                part = dot_rows(sketch[0], before[0])
            else:
                part = None
                for r in range(GROUP):
                    source = (me + GROUP - r) % GROUP
                    if r > 0:
                        gathers[r - 1].wait_recv()
                    columns = pl.ds(pl.multiple_of(source * width, 128), width)
                    term = dot_rows(last[source], before[0, :, columns])
                    part = term if part is None else part + term
            y_buf[idx, y] = part.astype(bf16)
            ready()
            own = y_buf.at[idx, y]
            factors = [remote(own, own, y_send.at[idx, r - 1], y_recv.at[idx, r - 1], y_peer(r)) for r in range(1, NY)]
            pending.extend(factors)
            if k > 0:
                gram = None
                for j in range(GROUP):
                    piece = last[j]
                    term = dot_rows(piece, jnp.concatenate([piece, piece], axis=0))
                    gram = term if gram is None else gram + term
                high = gram.astype(bf16).astype(f32)
                lane = lax.broadcasted_iota(jnp.int32, (RANK, 128), 1)
                g_buf[idx, y] = jnp.where(lane < RANK, high, gram - high).astype(bf16)
                own = g_buf.at[idx, y]
                grams = [
                    remote(own, own, g_send.at[idx, r - 1], g_recv.at[idx, r - 1], y_peer(r)) for r in range(1, NY)
                ]
                pending.extend(grams)
            yield

            for copy in factors:
                copy.wait_recv()
            token_sum = y_buf[idx, 0].astype(f32)
            for j in range(1, NY):
                token_sum = token_sum + y_buf[idx, j].astype(f32)
            rows = token_sum.astype(bf16)
            scatters = []
            for r in range(1, GROUP + 1):
                other = (me + r) % GROUP
                columns = pl.ds(pl.multiple_of(other * wide, 128), wide)
                piece = jnp.dot(rows, here[0, :, columns], preferred_element_type=f32).astype(bf16)
                if r == GROUP:
                    theirs[me] = piece
                else:
                    mine[other] = piece
                    scatters.append(
                        remote(
                            mine.at[other], theirs.at[me], rs_send.at[idx, r - 1], rs_recv.at[idx, r - 1],
                            group_peer(r),
                        )
                    )
            pending.extend(scatters)
            yield

            for copy in scatters:
                copy.wait_recv()
            total = theirs[0].astype(f32)
            for j in range(1, GROUP):
                total = total + theirs[j].astype(f32)
            z_b[0] = total.astype(bf16)
            exchange = remote(z_b.at[0], z_b.at[1], z_send.at[idx], z_recv.at[idx], z_peer)
            pending.append(exchange)
            yield

            if k > 0:
                for copy in grams:
                    copy.wait_recv()
                packed = g_buf[idx, 0].astype(f32)
                for j in range(1, NY):
                    packed = packed + g_buf[idx, j].astype(f32)
                gram = packed + pltpu.roll(packed, RANK, 1)
                line = lax.broadcasted_iota(jnp.int32, (RANK, 128), 0)
                lane = lax.broadcasted_iota(jnp.int32, (RANK, 128), 1)
                by_row = lax.rsqrt(jnp.sum(jnp.where(line == lane, gram, 0.0), axis=1, keepdims=True))
                diagonal = jnp.where((line == lane) | (line + RANK == lane), gram, 0.0)
                by_lane = lax.rsqrt(jnp.sum(diagonal, axis=0, keepdims=True))
                identity = jnp.where(line + RANK == lane, 1.0, 0.0)
                augmented = jnp.where(lane < RANK, gram * by_row * by_lane, identity)
                reduced = eliminate([augmented[8 * p : 8 * p + 8, :] for p in range(8)])
                for p in range(8):
                    inv_buf[c, 8 * p : 8 * p + 8, :] = reduced[p] * by_lane
                if k == STAGES - 1:
                    inverse = inv_buf[c][:, :RANK]
                    for j in range(GROUP):
                        basis = jnp.dot(
                            inverse, last[j].astype(f32), precision=precise, preferred_element_type=f32
                        )
                        b_out[0, :, j * width : (j + 1) * width] = (basis.astype(bf16).astype(f32) * 16.0).astype(bf16)
            yield

            exchange.wait_recv()
            total = z_b[0].astype(f32) + z_b[1].astype(f32)
            if k > 0:
                total = jnp.dot(inv_buf[c][:, :RANK], total, precision=precise, preferred_element_type=f32)
            total = total.astype(bf16)
            everyone[me] = total
            own = everyone.at[me]
            gathers = [
                remote(own, own, ag_send.at[idx, r - 1], ag_recv.at[idx, r - 1], group_peer(r))
                for r in range(1, GROUP)
            ]
            pending.extend(gathers)
            last = everyone
            if k == STAGES - 1:
                square = total.astype(f32)
                square = square * square
                energy = None
                for i in range(8):
                    for lanes in range(0, wide, 128):
                        term = square[8 * i : 8 * i + 8, lanes : lanes + 128]
                        energy = term if energy is None else energy + term
                e_buf[c, y] = energy
                own = e_buf.at[c, y]
                energies = [
                    remote(own, own, e_send.at[c, r - 1], e_recv.at[c, r - 1], y_peer(r)) for r in range(1, NY)
                ]
                pending.extend(energies)
            yield

        for copy in energies:
            copy.wait_recv()
        h_buf[c, me] = e_buf[c, 0] + e_buf[c, 1] + e_buf[c, 2] + e_buf[c, 3]
        own = h_buf.at[c, me]
        shares = [remote(own, own, h_send.at[c, r - 1], h_recv.at[c, r - 1], group_peer(r)) for r in range(1, GROUP)]
        pending.extend(shares)
        yield
        for copy in gathers + shares:
            copy.wait_recv()
        energy = h_buf[c, 0]
        for j in range(1, GROUP):
            energy = energy + h_buf[c, j]
        energy = jnp.sum(jnp.sum(energy, axis=1, keepdims=True), axis=0, keepdims=True)
        columns = GROUP * wide * NY
        factor = 1.0 / jnp.sqrt(energy / (RANK * columns) + 1e-06)
        for j in range(GROUP):
            a_out[0, :, j * wide : (j + 1) * wide] = last[j].astype(f32) * factor
        yield

    shifts = []

    def begin():
        if not shifts:
            pl.semaphore_wait(barrier, len(peers))
            shifts.append(remote(handed_hbm, up, up_sems.at[0], up_sems.at[1], {"section": behind}))
            pending.extend(shifts)

    loads[0].wait()
    loads[1].wait()
    chains = (
        chain(0, norm_ref, query_ref, sk_q_ref, b_q_ref, a_q_ref, begin),
        chain(1, attn_ref, up, sk_o_ref, b_o_ref, a_o_ref, begin),
    )
    next(chains[0])
    for load in loads[2:]:
        load.wait()
    for which in ORDER:
        if which == 2:
            shifts[0].wait_recv()
        else:
            next(chains[which])
    for copy in pending:
        copy.wait_send()


def body(*operands):
    norm_in, query_grad, attn_out, handed, sketch_q, sketch_o = operands
    dim, features = norm_in.shape[2], query_grad.shape[2]
    tokens = norm_in.shape[1]
    vmem = pl.BlockSpec(memory_space=pltpu.VMEM)
    wide, narrow = dim // GROUP, features // GROUP
    dma = pltpu.SemaphoreType.DMA
    n = 2 * STAGES
    out_shape = (
        jax.ShapeDtypeStruct((1, RANK, dim), bf16),
        jax.ShapeDtypeStruct((1, RANK, features), f32),
        jax.ShapeDtypeStruct((1, RANK, features), bf16),
        jax.ShapeDtypeStruct((1, RANK, dim), f32),
    )
    scratch = [
        pltpu.VMEM(norm_in.shape, bf16),
        pltpu.VMEM(query_grad.shape, bf16),
        pltpu.VMEM(attn_out.shape, bf16),
        pltpu.VMEM(sketch_q.shape, bf16),
        pltpu.VMEM(sketch_o.shape, bf16),
        pltpu.VMEM((1, tokens, dim), bf16),
        pltpu.VMEM((n, NY, RANK, 128), bf16),
        pltpu.VMEM((n, NY, RANK, 128), bf16),
        pltpu.VMEM((2, NY, 8, 128), f32),
        pltpu.VMEM((2, GROUP, 8, 128), f32),
        pltpu.VMEM((2, RANK, 128), f32),
        pltpu.VMEM((STAGES, GROUP, RANK, wide), bf16),
        pltpu.VMEM((STAGES, GROUP, RANK, narrow), bf16),
        pltpu.VMEM((STAGES, GROUP, RANK, wide), bf16),
        pltpu.VMEM((STAGES, GROUP, RANK, narrow), bf16),
        pltpu.VMEM((STAGES, 2, RANK, wide), bf16),
        pltpu.VMEM((STAGES, 2, RANK, narrow), bf16),
        pltpu.VMEM((STAGES, GROUP, RANK, wide), bf16),
        pltpu.VMEM((STAGES, GROUP, RANK, narrow), bf16),
        dma((2,)),
        dma((n, NY - 1)),
        dma((n, NY - 1)),
        dma((n, NY - 1)),
        dma((n, NY - 1)),
        dma((n, GROUP - 1)),
        dma((n, GROUP - 1)),
        dma((n,)),
        dma((n,)),
        dma((n, GROUP - 1)),
        dma((n, GROUP - 1)),
        dma((2, NY - 1)),
        dma((2, NY - 1)),
        dma((2, GROUP - 1)),
        dma((2, GROUP - 1)),
        dma((5,)),
    ]
    return pl.pallas_call(
        kernel,
        out_shape=out_shape,
        in_specs=[pl.BlockSpec(memory_space=pltpu.HBM)] * 6,
        out_specs=(vmem,) * 4,
        scratch_shapes=scratch,
        compiler_params=pltpu.CompilerParams(
            collective_id=0, has_side_effects=True, vmem_limit_bytes=65800000
        ),
        name="adapters",
    )(*operands)


def solution(mesh):
    row = P("section", "dp", "tensor")
    thin = P("section", None, "tensor")
    return jax.shard_map(
        body,
        mesh=mesh,
        in_specs=(row, row, row, row, thin, thin),
        out_specs=(thin, thin, thin, thin),
        check_vma=False,
    )
```

```python
import functools

import jax
import jax.numpy as jnp
from jax import lax
from jax.experimental import pallas as pl
from jax.experimental.pallas import tpu as pltpu
from jax.sharding import PartitionSpec as P

RANK = 64
POWER = 2
STAGES = 2 * POWER + 2
NY = 4
GROUP = 8
FAR = (4, 3, 5, 2, 6, 1, 7)
FAR_Y = (2, 1, 3)
MESH = pl.DeviceIdType.MESH
ORDER = [
    0, 0, 0, 2, 1, 1, 1, 0, 1, 0, 1, 0, 1, 0, 0, 1, 1, 0, 1, 0, 0, 1, 0, 1,
    0, 1, 1, 0, 1, 0, 1, 0, 1, 0, 0, 1, 1, 0, 1, 0, 0, 1, 0, 1, 0, 1, 1, 0,
    1, 0, 1, 0, 1, 0, 1, 0, 1, 0, 0, 1, 0, 1, 1, 1,
]
f32 = jnp.float32
bf16 = jnp.bfloat16
precise = lax.Precision.HIGHEST


def dot_rows(a, b):
    return lax.dot_general(a, b, (((1,), (1,)), ((), ())), preferred_element_type=f32)


def eliminate(blocks):
    sub = lax.broadcasted_iota(jnp.int32, (8, 128), 0)

    def across(value, i):
        return jnp.broadcast_to(value[:, i : i + 1], (8, 128))

    def down(value, i):
        return jnp.broadcast_to(value[i : i + 1, :], (8, 128))

    def one_block(b, rows):
        rows = list(rows)
        work = done = rows[0]
        columns = [across(work, i) for i in range(8)]
        for i in range(8):
            pivot = down(columns[i], i)
            root = lax.rsqrt(pivot)
            row = down(work, i)
            done = jnp.where(sub == i, row * root, done)
            step = jnp.where(sub == i, pivot - 1.0, columns[i]) * (root * root)
            for j in range(i + 1, 8):
                columns[j] = columns[j] - down(columns[j], i) * step
            work = work - row * step
        solved = [down(work, i) for i in range(8)]
        for p in range(1, 8):
            change = across(rows[p], 0) * solved[0]
            for i in range(1, 8):
                change = change + across(rows[p], i) * solved[i]
            live = jnp.where(p + b < 8, 1.0, 0.0).astype(f32)
            rows[p] = rows[p] - change * live
        rows[0] = done
        rows = [pltpu.roll(r, 120, 1) for r in rows]
        return tuple(rows[1:] + rows[:1])

    return lax.fori_loop(0, 8, one_block, tuple(blocks))


def kernel(
    norm_hbm, query_hbm, attn_hbm, handed_hbm, sk_q_hbm, sk_o_hbm,
    b_q_ref, a_q_ref, b_o_ref, a_o_ref,
    norm_ref, query_ref, attn_ref, sk_q_ref, sk_o_ref, up, y_buf, g_buf, e_buf, h_buf, inv_buf, send_w, send_n, recv_w, recv_n, z_w, z_n, all_w, all_n,
    up_sems, y_send, y_recv, g_send, g_recv, rs_send, rs_recv, z_send, z_recv, ag_send, ag_recv, e_send, e_recv, h_send, h_recv, in_sems,
):
    section = lax.axis_index("section")
    dp = lax.axis_index("dp")
    y = lax.axis_index("tensor")
    sections = lax.axis_size("section")
    x, z, core = dp // 4, (dp // 2) % 2, dp % 2
    me = x * 2 + core
    behind, ahead = (section + sections - 1) % sections, (section + 1) % sections

    def y_peer(r):
        return {"tensor": (y + r) % NY}

    def group_peer(r):
        other = (me + r) % GROUP
        return {"dp": ((other // 2) * 2 + z) * 2 + other % 2}

    z_peer = {"dp": (x * 2 + (1 - z)) * 2 + core}

    loads = [
        pltpu.make_async_copy(source, target, in_sems.at[i])
        for i, (source, target) in enumerate(
            (
                (query_hbm, query_ref), (sk_q_hbm, sk_q_ref), (norm_hbm, norm_ref),
                (sk_o_hbm, sk_o_ref), (attn_hbm, attn_ref),
            )
        )
    ]
    for load in loads:
        load.start()
    barrier = pltpu.get_barrier_semaphore()
    peers = [{"section": behind}, {"section": ahead}, z_peer]
    peers += [y_peer(r) for r in range(1, NY)] + [group_peer(r) for r in range(1, GROUP)]
    for peer in peers:
        pl.semaphore_signal(barrier, inc=1, device_id=peer, device_id_type=MESH)

    def remote(src, dst, sent, received, peer):
        copy = pltpu.make_async_remote_copy(
            src_ref=src, dst_ref=dst, send_sem=sent, recv_sem=received, device_id=peer, device_id_type=MESH
        )
        copy.start()
        return copy

    pending = []

    def chain(c, left, right, sketch, b_out, a_out, ready):
        for k in range(STAGES):
            before, here = (right, left) if k % 2 == 0 else (left, right)
            wide = here.shape[2] // GROUP
            width = before.shape[2] // GROUP
            slot = c * 3 + k // 2
            buffers = (send_w, recv_w, z_w, all_w) if wide == 256 else (send_n, recv_n, z_n, all_n)
            mine, theirs, z_b, everyone = (buffer.at[slot] for buffer in buffers)
            idx = c * STAGES + k

            if k == 0:
                part = dot_rows(sketch[0], before[0])
            else:
                part = None
                for r in (0,) + FAR[::-1]:
                    source = (me + GROUP - r) % GROUP
                    if r > 0:
                        gathers[FAR.index(r)].wait_recv()
                    columns = pl.ds(pl.multiple_of(source * width, 128), width)
                    term = dot_rows(last[source], before[0, :, columns])
                    part = term if part is None else part + term
            y_buf[idx, y] = part.astype(bf16)
            ready()
            own = y_buf.at[idx, y]
            factors = [remote(own, own, y_send.at[idx, r - 1], y_recv.at[idx, r - 1], y_peer(r)) for r in FAR_Y]
            pending.extend(factors)
            if k > 0:
                gram = None
                for j in range(GROUP):
                    piece = last[j]
                    term = dot_rows(piece, jnp.concatenate([piece, piece], axis=0))
                    gram = term if gram is None else gram + term
                high = gram.astype(bf16).astype(f32)
                lane = lax.broadcasted_iota(jnp.int32, (RANK, 128), 1)
                g_buf[idx, y] = jnp.where(lane < RANK, high, gram - high).astype(bf16)
                own = g_buf.at[idx, y]
                grams = [
                    remote(own, own, g_send.at[idx, r - 1], g_recv.at[idx, r - 1], y_peer(r)) for r in range(1, NY)
                ]
                pending.extend(grams)
            yield

            for copy in factors:
                copy.wait_recv()
            token_sum = y_buf[idx, 0].astype(f32)
            for j in range(1, NY):
                token_sum = token_sum + y_buf[idx, j].astype(f32)
            rows = token_sum.astype(bf16)
            scatters = []
            for r in FAR + (GROUP,):
                other = (me + r) % GROUP
                columns = pl.ds(pl.multiple_of(other * wide, 128), wide)
                piece = jnp.dot(rows, here[0, :, columns], preferred_element_type=f32).astype(bf16)
                if r == GROUP:
                    theirs[me] = piece
                else:
                    mine[other] = piece
                    scatters.append(
                        remote(
                            mine.at[other], theirs.at[me], rs_send.at[idx, r - 1], rs_recv.at[idx, r - 1],
                            group_peer(r),
                        )
                    )
            pending.extend(scatters)
            yield

            for copy in scatters:
                copy.wait_recv()
            total = theirs[0].astype(f32)
            for j in range(1, GROUP):
                total = total + theirs[j].astype(f32)
            z_b[0] = total.astype(bf16)
            exchange = remote(z_b.at[0], z_b.at[1], z_send.at[idx], z_recv.at[idx], z_peer)
            pending.append(exchange)
            yield

            if k > 0:
                for copy in grams:
                    copy.wait_recv()
                packed = g_buf[idx, 0].astype(f32)
                for j in range(1, NY):
                    packed = packed + g_buf[idx, j].astype(f32)
                gram = packed + pltpu.roll(packed, RANK, 1)
                line = lax.broadcasted_iota(jnp.int32, (RANK, 128), 0)
                lane = lax.broadcasted_iota(jnp.int32, (RANK, 128), 1)
                by_row = lax.rsqrt(jnp.sum(jnp.where(line == lane, gram, 0.0), axis=1, keepdims=True))
                diagonal = jnp.where((line == lane) | (line + RANK == lane), gram, 0.0)
                by_lane = lax.rsqrt(jnp.sum(diagonal, axis=0, keepdims=True))
                identity = jnp.where(line + RANK == lane, 1.0, 0.0)
                augmented = jnp.where(lane < RANK, gram * by_row * by_lane, identity)
                reduced = eliminate([augmented[8 * p : 8 * p + 8, :] for p in range(8)])
                for p in range(8):
                    inv_buf[c, 8 * p : 8 * p + 8, :] = reduced[p] * by_lane
                if k == STAGES - 1:
                    inverse = inv_buf[c][:, :RANK]
                    for j in range(GROUP):
                        basis = jnp.dot(
                            inverse, last[j].astype(f32), precision=precise, preferred_element_type=f32
                        )
                        b_out[0, :, j * width : (j + 1) * width] = (basis.astype(bf16).astype(f32) * 16.0).astype(bf16)
            yield

            exchange.wait_recv()
            total = z_b[0].astype(f32) + z_b[1].astype(f32)
            if k > 0:
                total = jnp.dot(inv_buf[c][:, :RANK], total, precision=precise, preferred_element_type=f32)
            total = total.astype(bf16)
            everyone[me] = total
            own = everyone.at[me]
            gathers = [
                remote(own, own, ag_send.at[idx, r - 1], ag_recv.at[idx, r - 1], group_peer(r))
                for r in FAR
            ]
            pending.extend(gathers)
            last = everyone
            if k == STAGES - 1:
                square = total.astype(f32)
                square = square * square
                energy = None
                for i in range(8):
                    for lanes in range(0, wide, 128):
                        term = square[8 * i : 8 * i + 8, lanes : lanes + 128]
                        energy = term if energy is None else energy + term
                e_buf[c, y] = energy
                own = e_buf.at[c, y]
                energies = [
                    remote(own, own, e_send.at[c, r - 1], e_recv.at[c, r - 1], y_peer(r)) for r in range(1, NY)
                ]
                pending.extend(energies)
            yield

        for copy in energies:
            copy.wait_recv()
        h_buf[c, me] = e_buf[c, 0] + e_buf[c, 1] + e_buf[c, 2] + e_buf[c, 3]
        own = h_buf.at[c, me]
        shares = [remote(own, own, h_send.at[c, r - 1], h_recv.at[c, r - 1], group_peer(r)) for r in range(1, GROUP)]
        pending.extend(shares)
        yield
        for copy in gathers + shares:
            copy.wait_recv()
        energy = h_buf[c, 0]
        for j in range(1, GROUP):
            energy = energy + h_buf[c, j]
        energy = jnp.sum(jnp.sum(energy, axis=1, keepdims=True), axis=0, keepdims=True)
        columns = GROUP * wide * NY
        factor = 1.0 / jnp.sqrt(energy / (RANK * columns) + 1e-06)
        for j in range(GROUP):
            a_out[0, :, j * wide : (j + 1) * wide] = last[j].astype(f32) * factor
        yield

    shifts = []

    def begin():
        if not shifts:
            pl.semaphore_wait(barrier, len(peers))
            shifts.append(remote(handed_hbm, up, up_sems.at[0], up_sems.at[1], {"section": behind}))
            pending.extend(shifts)

    loads[0].wait()
    loads[1].wait()
    chains = (
        chain(0, norm_ref, query_ref, sk_q_ref, b_q_ref, a_q_ref, begin),
        chain(1, attn_ref, up, sk_o_ref, b_o_ref, a_o_ref, begin),
    )
    next(chains[0])
    for load in loads[2:]:
        load.wait()
    for which in ORDER:
        if which == 2:
            shifts[0].wait_recv()
        else:
            next(chains[which])
    for copy in pending:
        copy.wait_send()


def body(*operands):
    norm_in, query_grad, attn_out, handed, sketch_q, sketch_o = operands
    dim, features = norm_in.shape[2], query_grad.shape[2]
    tokens = norm_in.shape[1]
    vmem = pl.BlockSpec(memory_space=pltpu.VMEM)
    wide, narrow = dim // GROUP, features // GROUP
    dma = pltpu.SemaphoreType.DMA
    n = 2 * STAGES
    out_shape = (
        jax.ShapeDtypeStruct((1, RANK, dim), bf16),
        jax.ShapeDtypeStruct((1, RANK, features), f32),
        jax.ShapeDtypeStruct((1, RANK, features), bf16),
        jax.ShapeDtypeStruct((1, RANK, dim), f32),
    )
    scratch = [
        pltpu.VMEM(norm_in.shape, bf16),
        pltpu.VMEM(query_grad.shape, bf16),
        pltpu.VMEM(attn_out.shape, bf16),
        pltpu.VMEM(sketch_q.shape, bf16),
        pltpu.VMEM(sketch_o.shape, bf16),
        pltpu.VMEM((1, tokens, dim), bf16),
        pltpu.VMEM((n, NY, RANK, 128), bf16),
        pltpu.VMEM((n, NY, RANK, 128), bf16),
        pltpu.VMEM((2, NY, 8, 128), f32),
        pltpu.VMEM((2, GROUP, 8, 128), f32),
        pltpu.VMEM((2, RANK, 128), f32),
        pltpu.VMEM((STAGES, GROUP, RANK, wide), bf16),
        pltpu.VMEM((STAGES, GROUP, RANK, narrow), bf16),
        pltpu.VMEM((STAGES, GROUP, RANK, wide), bf16),
        pltpu.VMEM((STAGES, GROUP, RANK, narrow), bf16),
        pltpu.VMEM((STAGES, 2, RANK, wide), bf16),
        pltpu.VMEM((STAGES, 2, RANK, narrow), bf16),
        pltpu.VMEM((STAGES, GROUP, RANK, wide), bf16),
        pltpu.VMEM((STAGES, GROUP, RANK, narrow), bf16),
        dma((2,)),
        dma((n, NY - 1)),
        dma((n, NY - 1)),
        dma((n, NY - 1)),
        dma((n, NY - 1)),
        dma((n, GROUP - 1)),
        dma((n, GROUP - 1)),
        dma((n,)),
        dma((n,)),
        dma((n, GROUP - 1)),
        dma((n, GROUP - 1)),
        dma((2, NY - 1)),
        dma((2, NY - 1)),
        dma((2, GROUP - 1)),
        dma((2, GROUP - 1)),
        dma((5,)),
    ]
    return pl.pallas_call(
        kernel,
        out_shape=out_shape,
        in_specs=[pl.BlockSpec(memory_space=pltpu.HBM)] * 6,
        out_specs=(vmem,) * 4,
        scratch_shapes=scratch,
        compiler_params=pltpu.CompilerParams(
            collective_id=0, has_side_effects=True, vmem_limit_bytes=65800000
        ),
        name="adapters",
    )(*operands)


def solution(mesh):
    row = P("section", "dp", "tensor")
    thin = P("section", None, "tensor")
    return jax.shard_map(
        body,
        mesh=mesh,
        in_specs=(row, row, row, row, thin, thin),
        out_specs=(thin, thin, thin, thin),
        check_vma=False,
    )
```
